32 devices in a mesh: row: 2 (over y), pair: 16 (over z, x, core).
Axes of the slice: x: 2, y: 2, z: 4, core: 2. Of those that a mesh axis runs over, the one named last changes fastest.
Arguments:
- panel: float32 [4096, 4096], P('row', 'pair'), may hold values from -51 to 51
- slot_block: int32 [32], replicated, may hold values from 0 to 31, each once
Outputs:
- rotated: float32 [4096, 4096], P('row', 'pair')
The draws below stay inside these ranges and needn't reach their ends.
Inputs may be any that keep to these rules, and one draw needn't show every extreme that they name: `slot_block`: each block number appears once.
All inputs are finite; a program needn't handle non-finite values.
Results may differ from the reference program's by a relative error of at most 0.0003.
Values sent between devices are 32-bit elements; how exact they have to be, the bound alone decides.
A program may use at most 64 MiB of HBM per device.

```python
import math
import jax
import jax.numpy as jnp
from jax import lax

B = 128
STEPS = 2
NS_ITERS = 3
PAIRS = 16
SLOTS = 32
NCOL = 4096
M = 4096


def draw_panel(key, part):
    keys = jax.random.split(jax.random.fold_in(key, 7), 3)
    base = jnp.clip(jax.random.normal(keys[0], (M, NCOL), jnp.float32), -6.0, 6.0)
    row_scale = jnp.exp(jax.random.uniform(keys[1], (M, 1), jnp.float32, math.log(0.3), math.log(3.0)))
    col_scale = jnp.exp(jax.random.uniform(keys[2], (1, NCOL), jnp.float32, math.log(0.5), math.log(2.0)))
    return base * row_scale * col_scale


def setup_inputs(seed: int = 0) -> dict:
    seeds = jax.random.split(jax.random.key(seed), 3)
    panel = draw_panel(jax.random.fold_in(seeds[2], 71), 0)
    slot_block = jax.random.permutation(seeds[1], SLOTS).astype(jnp.int32)
    return {"panel": panel, "slot_block": slot_block}


precise = lax.Precision.HIGHEST

def inverse_root(matrix):
    identity = jnp.eye(matrix.shape[0], dtype=matrix.dtype)
    approx = matrix
    root_inv = identity
    for sweep in range(NS_ITERS):
        factor = 1.5 * identity - 0.5 * jnp.dot(root_inv, approx, precision=precise)
        approx = jnp.dot(approx, factor, precision=precise)
        root_inv = jnp.dot(factor, root_inv, precision=precise)
    return root_inv / jnp.sqrt(5.0)

def couple(cross):
    identity = jnp.eye(cross.shape[0], dtype=cross.dtype)
    coupling = cross * (2.0 / jnp.sqrt(jnp.sum(cross * cross) + 1e-06))
    left = (identity + jnp.dot(coupling, coupling.T, precision=precise)) / 5.0
    right = (identity + jnp.dot(coupling.T, coupling, precision=precise)) / 5.0
    return (coupling, left, right)

def apply_rotation(first, second, coupling, left_inverse, right_inverse):
    new_first = jnp.dot(first + jnp.dot(second, coupling.T, precision=precise), left_inverse, precision=precise)
    new_second = jnp.dot(second - jnp.dot(first, coupling, precision=precise), right_inverse, precision=precise)
    return (new_first, new_second)

def move_slots(uppers, lowers):
    new_uppers = jnp.concatenate([uppers[0:1], lowers[0:1], uppers[1:-1]], axis=0)
    new_lowers = jnp.concatenate([lowers[1:], uppers[-1:]], axis=0)
    return (new_uppers, new_lowers)

def one_pair(items):
    upper, lower, upper_id, lower_id = items
    order_flag = upper_id < lower_id
    first = jnp.where(order_flag, upper, lower)
    second = jnp.where(order_flag, lower, upper)
    cross = jnp.dot(first.T, second, precision=precise)
    coupling, left, right = couple(cross)
    new_first, new_second = apply_rotation(first, second, coupling, inverse_root(left), inverse_root(right))
    return (jnp.where(order_flag, new_first, new_second), jnp.where(order_flag, new_second, new_first))

def reference(panel, slot_block):
    blocks = panel.reshape(M, PAIRS, 2, B)
    uppers = jnp.transpose(blocks[:, :, 0, :], (1, 0, 2))
    lowers = jnp.transpose(blocks[:, :, 1, :], (1, 0, 2))
    upper_ids = slot_block[:PAIRS]
    lower_ids = slot_block[PAIRS:]
    for step in range(STEPS):
        uppers, lowers = lax.map(one_pair, (uppers, lowers, upper_ids, lower_ids))
        uppers, lowers = move_slots(uppers, lowers)
        upper_ids, lower_ids = move_slots(upper_ids, lower_ids)
    stacked = jnp.stack([uppers, lowers], axis=1)
    return jnp.transpose(stacked, (2, 0, 1, 3)).reshape(M, NCOL)
```

```python
import functools
import math

import jax
import jax.numpy as jnp
from jax import lax
from jax.experimental import pallas as pl
from jax.experimental.pallas import tpu as pltpu
from jax.sharding import PartitionSpec as P

STEPS = 2
NS_ITERS = 3
CHUNKS = 8
MESH = pl.DeviceIdType.MESH
F32 = jnp.float32
BF16 = jnp.bfloat16


def split(value):
    high = value.astype(BF16)
    return high, (value - high.astype(F32)).astype(BF16)


def raw_dot(a, b):
    return jnp.dot(a, b, preferred_element_type=F32)


def product(a, b):
    (a_high, a_low), (b_high, b_low) = a, b
    return raw_dot(a_high, b_high) + (raw_dot(a_high, b_low) + raw_dot(a_low, b_high))


def inner_rows(upper, lower):
    width = upper.shape[1]
    both = lax.dot_general(
        jnp.concatenate(split(upper), axis=1),
        jnp.concatenate(split(lower), axis=1),
        (((0,), (0,)), ((), ())),
        preferred_element_type=F32,
    )
    small = both[:width, width:] + both[width:, :width] + both[width:, width:]
    return both[:width, :width] + small


def identity_of(size):
    rows = lax.broadcasted_iota(jnp.int32, (size, size), 0)
    columns = lax.broadcasted_iota(jnp.int32, (size, size), 1)
    return jnp.where(rows == columns, 1.0, 0.0).astype(F32)


def inverse_root(matrix, identity):
    factor = 1.5 * identity - 0.5 * matrix
    root_inv = factor
    approx = matrix
    for sweep in range(1, NS_ITERS):
        factor_parts = split(factor)
        approx = product(split(approx), factor_parts)
        root_parts = split(root_inv)
        factor = 1.5 * identity - 0.5 * product(root_parts, split(approx))
        root_inv = product(split(factor), root_parts)
    return root_inv * (1.0 / math.sqrt(5.0))


def rotation(cross, sign):
    identity = identity_of(cross.shape[0])
    coupling = cross * (sign * (2.0 * lax.rsqrt(jnp.sum(cross * cross, keepdims=True) + 1e-06)))
    turned = coupling.T
    coupling_parts, turned_parts = split(coupling), split(turned)
    left = (identity + product(coupling_parts, turned_parts)) * 0.2
    right = (identity + product(turned_parts, coupling_parts)) * 0.2
    left_inverse = inverse_root(left, identity)
    right_inverse = inverse_root(right, identity)
    from_lower = product(turned_parts, split(left_inverse))
    from_upper = -product(coupling_parts, split(right_inverse))
    return jnp.concatenate(
        [
            jnp.concatenate([left_inverse, from_upper], axis=1),
            jnp.concatenate([from_lower, right_inverse], axis=1),
        ],
        axis=0,
    )


def kernel(
    rows_axis, pairs, ids, panel, out,
    start, uppers, lowers, to_right, to_left, weights, crosses,
    load_sem, cross_send, cross_recv, right_send, right_recv, left_send, left_recv, keep_sem,
):
    width = panel.shape[1] // 2
    chunk = panel.shape[0] // CHUNKS
    position = lax.axis_index("pair")
    row = lax.axis_index("row")
    first, last = position == 0, position == pairs - 1
    right, left = lax.rem(position + 1, pairs), lax.rem(position + pairs - 1, pairs)

    def load(index):
        return pltpu.make_async_copy(
            panel.at[pl.ds(index * chunk, chunk), :], start.at[index], load_sem.at[index]
        )

    def start_load(index, carry):
        load(index).start()
        return carry

    lax.fori_loop(0, CHUNKS, start_load, 0)

    barrier = pltpu.get_barrier_semaphore()
    for offset in range(1, rows_axis):
        peer = lax.rem(row + offset, rows_axis)
        pl.semaphore_signal(barrier, inc=1, device_id={"row": peer}, device_id_type=MESH)

    @pl.when(jnp.logical_not(first))
    def _():
        pl.semaphore_signal(barrier, inc=1, device_id={"pair": left}, device_id_type=MESH)

    @pl.when(jnp.logical_not(last))
    def _():
        pl.semaphore_signal(barrier, inc=1, device_id={"pair": right}, device_id_type=MESH)

    def sign_of(upper_id, lower_id):
        return jnp.where(upper_id < lower_id, 1.0, -1.0).astype(F32)

    moved_upper = jnp.where(first, ids[0], jnp.where(position == 1, ids[pairs], ids[left]))
    moved_lower = jnp.where(last, ids[pairs - 1], ids[pairs + right])
    signs = (
        sign_of(ids[position], ids[pairs + position]),
        sign_of(moved_upper, moved_lower),
    )

    def send_right(step, index):
        if step == 0:
            target = uppers.at[index]
        else:
            target = out.at[pl.ds(index * chunk, chunk), pl.ds(0, width)]
        return pltpu.make_async_remote_copy(
            src_ref=to_right.at[step, index],
            dst_ref=target,
            send_sem=right_send.at[step, index],
            recv_sem=right_recv.at[step, index],
            device_id={"pair": right},
            device_id_type=MESH,
        )

    def send_left(step, index):
        if step == 0:
            target = lowers.at[index]
        else:
            target = out.at[pl.ds(index * chunk, chunk), pl.ds(width, width)]
        return pltpu.make_async_remote_copy(
            src_ref=to_left.at[step, index],
            dst_ref=target,
            send_sem=left_send.at[step, index],
            recv_sem=left_recv.at[step, index],
            device_id={"pair": left},
            device_id_type=MESH,
        )

    def keep_upper(index):
        return pltpu.make_async_copy(
            uppers.at[index],
            out.at[pl.ds(index * chunk, chunk), pl.ds(0, width)],
            keep_sem.at[index],
        )

    def keep_lower(index):
        return pltpu.make_async_copy(
            lowers.at[index],
            out.at[pl.ds(index * chunk, chunk), pl.ds(width, width)],
            keep_sem.at[index],
        )

    def exchange(step, offset):
        peer = lax.rem(row + offset, rows_axis)
        return pltpu.make_async_remote_copy(
            src_ref=crosses.at[step, row],
            dst_ref=crosses.at[step, row],
            send_sem=cross_send.at[step, offset - 1],
            recv_sem=cross_recv.at[step, offset - 1],
            device_id={"row": peer},
            device_id_type=MESH,
        )

    for step in range(STEPS):

        def halves(index):
            if step == 0:
                return start[index, :, :width], start[index, :, width:]
            return uppers[index], lowers[index]

        def add_chunk(index, total):
            if step == 0:
                load(index).wait()
            else:

                @pl.when(jnp.logical_not(first))
                def _():
                    send_right(0, index).wait_recv()

                @pl.when(jnp.logical_not(last))
                def _():
                    send_left(0, index).wait_recv()

            return total + inner_rows(*halves(index))

        total = lax.fori_loop(0, CHUNKS, add_chunk, jnp.zeros((width, width), F32))
        crosses[step, row] = total
        if step == 0:
            neighbours = jnp.where(first, 0, 1) + jnp.where(last, 0, 1)
            pl.semaphore_wait(barrier, rows_axis - 1 + neighbours)
        copies = [exchange(step, offset) for offset in range(1, rows_axis)]
        for copy in copies:
            copy.start()
        for copy in copies:
            copy.wait()
        cross = crosses[step, 0]
        for index in range(1, rows_axis):
            cross = cross + crosses[step, index]
        for part, value in enumerate(split(rotation(cross, signs[step]))):
            weights[part] = value

        def turn_chunk(index, carry):
            upper, lower = halves(index)
            parts = split(jnp.concatenate([upper, lower], axis=1))
            turned = product(parts, (weights[0], weights[1]))
            new_upper, new_lower = turned[:, :width], turned[:, width:]
            to_right[step, index] = jnp.where(first, new_lower, new_upper)
            to_left[step, index] = new_lower

            @pl.when(jnp.logical_not(last))
            def _():
                send_right(step, index).start()

            @pl.when(jnp.logical_not(first))
            def _():
                send_left(step, index).start()

            @pl.when(first)
            def _():
                uppers[index] = new_upper
                if step == STEPS - 1:
                    keep_upper(index).start()

            @pl.when(last)
            def _():
                lowers[index] = new_upper
                if step == STEPS - 1:
                    keep_lower(index).start()

            return carry

        lax.fori_loop(0, CHUNKS, turn_chunk, 0)

    def finish(index, carry):
        @pl.when(jnp.logical_not(last))
        def _():
            send_right(0, index).wait_send()
            send_right(1, index).wait_send()
            send_left(1, index).wait_recv()

        @pl.when(jnp.logical_not(first))
        def _():
            send_left(0, index).wait_send()
            send_left(1, index).wait_send()
            send_right(1, index).wait_recv()

        @pl.when(first)
        def _():
            keep_upper(index).wait()

        @pl.when(last)
        def _():
            keep_lower(index).wait()

        return carry

    lax.fori_loop(0, CHUNKS, finish, 0)


def solution(mesh):
    rows_axis, pairs = mesh.shape["row"], mesh.shape["pair"]

    def per_device(panel, slot_block):
        rows, width = panel.shape[0], panel.shape[1] // 2
        chunk = rows // CHUNKS
        dma = pltpu.SemaphoreType.DMA
        return pl.pallas_call(
            functools.partial(kernel, rows_axis, pairs),
            out_shape=jax.ShapeDtypeStruct(panel.shape, panel.dtype),
            in_specs=[
                pl.BlockSpec(memory_space=pltpu.SMEM),
                pl.BlockSpec(memory_space=pl.ANY),
            ],
            out_specs=pl.BlockSpec(memory_space=pl.ANY),
            scratch_shapes=[
                pltpu.VMEM((CHUNKS, chunk, 2 * width), F32),
                pltpu.VMEM((CHUNKS, chunk, width), F32),
                pltpu.VMEM((CHUNKS, chunk, width), F32),
                pltpu.VMEM((STEPS, CHUNKS, chunk, width), F32),
                pltpu.VMEM((STEPS, CHUNKS, chunk, width), F32),
                pltpu.VMEM((2, 2 * width, 2 * width), BF16),
                pltpu.VMEM((STEPS, rows_axis, width, width), F32),
                dma((CHUNKS,)),
                dma((STEPS, max(1, rows_axis - 1))),
                dma((STEPS, max(1, rows_axis - 1))),
                dma((STEPS, CHUNKS)),
                dma((STEPS, CHUNKS)),
                dma((STEPS, CHUNKS)),
                dma((STEPS, CHUNKS)),
                dma((CHUNKS,)),
            ],
            compiler_params=pltpu.CompilerParams(collective_id=0, has_side_effects=True),
        )(slot_block, panel)

    return jax.shard_map(
        per_device,
        mesh=mesh,
        in_specs=(P("row", "pair"), P()),
        out_specs=P("row", "pair"),
        check_vma=False,
    )
```

```python
import functools
import math

import jax
import jax.numpy as jnp
from jax import lax
from jax.experimental import pallas as pl
from jax.experimental.pallas import tpu as pltpu
from jax.sharding import PartitionSpec as P

STEPS = 2
NS_ITERS = 3
CHUNKS = 8
MESH = pl.DeviceIdType.MESH
F32 = jnp.float32
BF16 = jnp.bfloat16


def split(value):
    high = value.astype(BF16)
    return high, (value - high.astype(F32)).astype(BF16)


def raw_dot(a, b):
    return jnp.dot(a, b, preferred_element_type=F32)


def product(a, b):
    (a_high, a_low), (b_high, b_low) = a, b
    return raw_dot(a_high, b_high) + (raw_dot(a_high, b_low) + raw_dot(a_low, b_high))


def inner_rows(upper, lower):
    width = upper.shape[1]
    both = lax.dot_general(
        jnp.concatenate(split(upper), axis=1),
        jnp.concatenate(split(lower), axis=1),
        (((0,), (0,)), ((), ())),
        preferred_element_type=F32,
    )
    small = both[:width, width:] + both[width:, :width] + both[width:, width:]
    return both[:width, :width] + small


def identity_of(size):
    rows = lax.broadcasted_iota(jnp.int32, (size, size), 0)
    columns = lax.broadcasted_iota(jnp.int32, (size, size), 1)
    return jnp.where(rows == columns, 1.0, 0.0).astype(F32)


def inverse_root(matrix, identity):
    factor = 1.5 * identity - 0.5 * matrix
    root_inv = factor
    approx = matrix
    for sweep in range(1, NS_ITERS):
        factor_parts = split(factor)
        approx = product(split(approx), factor_parts)
        root_parts = split(root_inv)
        factor = 1.5 * identity - 0.5 * product(root_parts, split(approx))
        root_inv = product(split(factor), root_parts)
    return root_inv * (1.0 / math.sqrt(5.0))


def rotation(cross, sign):
    identity = identity_of(cross.shape[0])
    coupling = cross * (sign * (2.0 * lax.rsqrt(jnp.sum(cross * cross, keepdims=True) + 1e-06)))
    turned = coupling.T
    coupling_parts, turned_parts = split(coupling), split(turned)
    left = (identity + product(coupling_parts, turned_parts)) * 0.2
    right = (identity + product(turned_parts, coupling_parts)) * 0.2
    left_inverse = inverse_root(left, identity)
    right_inverse = inverse_root(right, identity)
    from_lower = product(turned_parts, split(left_inverse))
    from_upper = -product(coupling_parts, split(right_inverse))
    return jnp.concatenate(
        [
            jnp.concatenate([left_inverse, from_upper], axis=1),
            jnp.concatenate([from_lower, right_inverse], axis=1),
        ],
        axis=0,
    )


def kernel(
    rows_axis, pairs, ids, panel, out,
    start, uppers, lowers, to_right, to_left, weights, crosses,
    load_sem, cross_send, cross_recv, right_send, right_recv, left_send, left_recv, turn_sem,
):
    width = panel.shape[1] // 2
    chunk = panel.shape[0] // CHUNKS
    position = lax.axis_index("pair")
    row = lax.axis_index("row")
    first, last = position == 0, position == pairs - 1
    odd = lax.rem(position, 2) == 1
    right, left = lax.rem(position + 1, pairs), lax.rem(position + pairs - 1, pairs)

    def load(index):
        return pltpu.make_async_copy(
            panel.at[pl.ds(index * chunk, chunk), :], start.at[index], load_sem.at[index]
        )

    def start_load(index, carry):
        load(index).start()
        return carry

    lax.fori_loop(0, CHUNKS, start_load, 0)

    barrier = pltpu.get_barrier_semaphore()
    for offset in range(1, rows_axis):
        peer = lax.rem(row + offset, rows_axis)
        pl.semaphore_signal(barrier, inc=1, device_id={"row": peer}, device_id_type=MESH)

    @pl.when(jnp.logical_not(first))
    def _():
        pl.semaphore_signal(barrier, inc=1, device_id={"pair": left}, device_id_type=MESH)

    @pl.when(jnp.logical_not(last))
    def _():
        pl.semaphore_signal(barrier, inc=1, device_id={"pair": right}, device_id_type=MESH)

    def sign_of(upper_id, lower_id):
        return jnp.where(upper_id < lower_id, 1.0, -1.0).astype(F32)

    moved_upper = jnp.where(first, ids[0], jnp.where(position == 1, ids[pairs], ids[left]))
    moved_lower = jnp.where(last, ids[pairs - 1], ids[pairs + right])
    signs = (
        sign_of(ids[position], ids[pairs + position]),
        sign_of(moved_upper, moved_lower),
    )

    def send_right(step, index):
        if step == 0:
            target = uppers.at[index]
        else:
            target = out.at[pl.ds(index * chunk, chunk), pl.ds(0, width)]
        return pltpu.make_async_remote_copy(
            src_ref=to_right.at[step, index],
            dst_ref=target,
            send_sem=right_send.at[step, index],
            recv_sem=right_recv.at[step, index],
            device_id={"pair": right},
            device_id_type=MESH,
        )

    def send_left(step, index):
        if step == 0:
            target = lowers.at[index]
        else:
            target = out.at[pl.ds(index * chunk, chunk), pl.ds(width, width)]
        return pltpu.make_async_remote_copy(
            src_ref=to_left.at[step, index],
            dst_ref=target,
            send_sem=left_send.at[step, index],
            recv_sem=left_recv.at[step, index],
            device_id={"pair": left},
            device_id_type=MESH,
        )

    def exchange(step, offset):
        peer = lax.rem(row + offset, rows_axis)
        return pltpu.make_async_remote_copy(
            src_ref=crosses.at[step, row],
            dst_ref=crosses.at[step, row],
            send_sem=cross_send.at[step, offset - 1],
            recv_sem=cross_recv.at[step, offset - 1],
            device_id={"row": peer},
            device_id_type=MESH,
        )

    def start_left(index, carry):
        send_left(0, index).start()
        return carry

    def end_right(index, carry):
        send_right(0, index).wait_send()
        return carry

    for step in range(STEPS):

        def halves(index):
            if step == 0:
                return start[index, :, :width], start[index, :, width:]
            return uppers[index], lowers[index]

        def add_chunk(index, total):
            if step == 0:
                load(index).wait()
            else:

                @pl.when(jnp.logical_not(first))
                def _():
                    send_right(0, index).wait_recv()

                @pl.when(jnp.logical_not(last))
                def _():
                    send_left(0, index).wait_recv()

            return total + inner_rows(*halves(index))

        total = lax.fori_loop(0, CHUNKS - 1, add_chunk, jnp.zeros((width, width), F32))
        if step == 1:
            @pl.when(jnp.logical_not(odd))
            def _():
                pl.semaphore_wait(turn_sem, 1)

                @pl.when(jnp.logical_not(first))
                def _():
                    lax.fori_loop(0, CHUNKS, start_left, 0)

        total = add_chunk(CHUNKS - 1, total)
        crosses[step, row] = total
        if step == 0:
            neighbours = jnp.where(first, 0, 1) + jnp.where(last, 0, 1)
            pl.semaphore_wait(barrier, rows_axis - 1 + neighbours)
        copies = [exchange(step, offset) for offset in range(1, rows_axis)]
        for copy in copies:
            copy.start()
        for copy in copies:
            copy.wait()
        cross = crosses[step, 0]
        for index in range(1, rows_axis):
            cross = cross + crosses[step, index]
        for part, value in enumerate(split(rotation(cross, signs[step]))):
            weights[part] = value

        def turn_chunk(index, carry):
            upper, lower = halves(index)
            parts = split(jnp.concatenate([upper, lower], axis=1))
            turned = product(parts, (weights[0], weights[1]))
            new_upper, new_lower = turned[:, :width], turned[:, width:]
            to_right[step, index] = jnp.where(first, new_lower, new_upper)
            to_left[step, index] = new_lower

            @pl.when(jnp.logical_not(last))
            def _():
                send_right(step, index).start()

            @pl.when(odd if step == 0 else jnp.logical_not(first))
            def _():
                send_left(step, index).start()

            @pl.when(first)
            def _():
                if step == STEPS - 1:
                    out[pl.ds(index * chunk, chunk), :width] = new_upper
                else:
                    uppers[index] = new_upper

            @pl.when(last)
            def _():
                if step == STEPS - 1:
                    out[pl.ds(index * chunk, chunk), width:] = new_upper
                else:
                    lowers[index] = new_upper

            return carry

        lax.fori_loop(0, CHUNKS, turn_chunk, 0)
        if step == 0:

            @pl.when(odd)
            def _():
                @pl.when(jnp.logical_not(last))
                def _():
                    lax.fori_loop(0, CHUNKS - 1, end_right, 0)

                pl.semaphore_signal(turn_sem, inc=1, device_id={"pair": left}, device_id_type=MESH)

                @pl.when(jnp.logical_not(last))
                def _():
                    end_right(CHUNKS - 1, 0)

    def finish(index, carry):
        @pl.when(jnp.logical_not(last))
        def _():
            @pl.when(jnp.logical_not(odd))
            def _():
                send_right(0, index).wait_send()

            send_right(1, index).wait_send()
            send_left(1, index).wait_recv()

        @pl.when(jnp.logical_not(first))
        def _():
            send_left(0, index).wait_send()
            send_left(1, index).wait_send()
            send_right(1, index).wait_recv()

        return carry

    lax.fori_loop(0, CHUNKS, finish, 0)


def solution(mesh):
    rows_axis, pairs = mesh.shape["row"], mesh.shape["pair"]

    def per_device(panel, slot_block):
        rows, width = panel.shape[0], panel.shape[1] // 2
        chunk = rows // CHUNKS
        dma = pltpu.SemaphoreType.DMA
        return pl.pallas_call(
            functools.partial(kernel, rows_axis, pairs),
            out_shape=jax.ShapeDtypeStruct(panel.shape, panel.dtype),
            in_specs=[
                pl.BlockSpec(memory_space=pltpu.SMEM),
                pl.BlockSpec(memory_space=pltpu.HBM),
            ],
            out_specs=pl.BlockSpec(memory_space=pltpu.VMEM),
            scratch_shapes=[
                pltpu.VMEM((CHUNKS, chunk, 2 * width), F32),
                pltpu.VMEM((CHUNKS, chunk, width), F32),
                pltpu.VMEM((CHUNKS, chunk, width), F32),
                pltpu.VMEM((STEPS, CHUNKS, chunk, width), F32),
                pltpu.VMEM((STEPS, CHUNKS, chunk, width), F32),
                pltpu.VMEM((2, 2 * width, 2 * width), BF16),
                pltpu.VMEM((STEPS, rows_axis, width, width), F32),
                dma((CHUNKS,)),
                dma((STEPS, max(1, rows_axis - 1))),
                dma((STEPS, max(1, rows_axis - 1))),
                dma((STEPS, CHUNKS)),
                dma((STEPS, CHUNKS)),
                dma((STEPS, CHUNKS)),
                dma((STEPS, CHUNKS)),
                pltpu.SemaphoreType.REGULAR,
            ],
            compiler_params=pltpu.CompilerParams(collective_id=0, has_side_effects=True, vmem_limit_bytes=10 * panel.size * 4),
        )(slot_block, panel)

    return jax.shard_map(
        per_device,
        mesh=mesh,
        in_specs=(P("row", "pair"), P()),
        out_specs=P("row", "pair"),
        check_vma=False,
    )
```

```python
import functools
import math

import jax
import jax.numpy as jnp
from jax import lax
from jax.experimental import pallas as pl
from jax.experimental.pallas import tpu as pltpu
from jax.sharding import PartitionSpec as P

STEPS = 2
NS_ITERS = 3
CHUNKS = 8
MESH = pl.DeviceIdType.MESH
F32 = jnp.float32
BF16 = jnp.bfloat16


def split(value):
    high = value.astype(BF16)
    return high, (value - high.astype(F32)).astype(BF16)


def raw_dot(a, b):
    return jnp.dot(a, b, preferred_element_type=F32)


def product(a, b):
    (a_high, a_low), (b_high, b_low) = a, b
    return raw_dot(a_high, b_high) + (raw_dot(a_high, b_low) + raw_dot(a_low, b_high))


def inner_rows(upper, lower):
    width = upper.shape[1]
    both = lax.dot_general(
        jnp.concatenate(split(upper), axis=1),
        jnp.concatenate(split(lower), axis=1),
        (((0,), (0,)), ((), ())),
        preferred_element_type=F32,
    )
    small = both[:width, width:] + both[width:, :width] + both[width:, width:]
    return both[:width, :width] + small


def identity_of(size):
    rows = lax.broadcasted_iota(jnp.int32, (size, size), 0)
    columns = lax.broadcasted_iota(jnp.int32, (size, size), 1)
    return jnp.where(rows == columns, 1.0, 0.0).astype(F32)


def rotation(cross, sign):
    identity = identity_of(cross.shape[0])
    scale = 2.0 * lax.rsqrt(jnp.sum(cross * cross, keepdims=True) + 1e-06)
    turned = cross.T
    plain_parts, turned_parts = split(cross), split(turned)
    sides = ((plain_parts, turned_parts), (turned_parts, plain_parts))
    iterates = [0.2 * identity + (0.2 * scale * scale) * product(a, b) for a, b in sides]
    factors = [1.5 * identity - 0.5 * value for value in iterates]
    roots = list(factors)
    for sweep in range(1, NS_ITERS):
        parts = [split(value) for value in factors]
        squares = [product(value, value) for value in parts]
        iterates = [product(split(a), split(b)) for a, b in zip(iterates, squares)]
        factors = [1.5 * identity - 0.5 * value for value in iterates]
        if sweep < NS_ITERS - 1:
            roots = [product(split(a), split(b)) for a, b in zip(roots, factors)]
    root_parts = [split(value * (1.0 / math.sqrt(5.0))) for value in roots]
    mixed = [
        split((sign * scale) * product(turned_parts, root_parts[0])),
        split((-sign * scale) * product(plain_parts, root_parts[1])),
    ]
    last_parts = [split(value) for value in factors]
    left_inverse, right_inverse = (product(a, b) for a, b in zip(root_parts, last_parts))
    from_lower, from_upper = (product(a, b) for a, b in zip(mixed, last_parts))
    return jnp.concatenate(
        [
            jnp.concatenate([left_inverse, from_upper], axis=1),
            jnp.concatenate([from_lower, right_inverse], axis=1),
        ],
        axis=0,
    )


def kernel(
    rows_axis, pairs, ids, panel, out,
    start, uppers, lowers, to_right, to_left, weights, crosses,
    load_sem, cross_send, cross_recv, right_send, right_recv, left_send, left_recv, turn_sem, first_sem,
):
    width = panel.shape[1] // 2
    chunk = panel.shape[0] // CHUNKS
    position = lax.axis_index("pair")
    row = lax.axis_index("row")
    first, last = position == 0, position == pairs - 1
    odd = lax.rem(position, 2) == 1
    right, left = lax.rem(position + 1, pairs), lax.rem(position + pairs - 1, pairs)

    def load(index):
        return pltpu.make_async_copy(
            panel.at[pl.ds(index * chunk, chunk), :], start.at[index], load_sem.at[index]
        )

    def start_load(index, carry):
        load(index).start()
        return carry

    lax.fori_loop(0, CHUNKS, start_load, 0)

    barrier = pltpu.get_barrier_semaphore()
    for offset in range(1, rows_axis):
        peer = lax.rem(row + offset, rows_axis)
        pl.semaphore_signal(barrier, inc=1, device_id={"row": peer}, device_id_type=MESH)

    @pl.when(jnp.logical_not(first))
    def _():
        pl.semaphore_signal(barrier, inc=1, device_id={"pair": left}, device_id_type=MESH)

    @pl.when(jnp.logical_not(last))
    def _():
        pl.semaphore_signal(barrier, inc=1, device_id={"pair": right}, device_id_type=MESH)

    def sign_of(upper_id, lower_id):
        return jnp.where(upper_id < lower_id, 1.0, -1.0).astype(F32)

    moved_upper = jnp.where(first, ids[0], jnp.where(position == 1, ids[pairs], ids[left]))
    moved_lower = jnp.where(last, ids[pairs - 1], ids[pairs + right])
    signs = (
        sign_of(ids[position], ids[pairs + position]),
        sign_of(moved_upper, moved_lower),
    )

    def send_right(step, index):
        if step == 0:
            target = uppers.at[index]
        else:
            target = out.at[pl.ds(index * chunk, chunk), pl.ds(0, width)]
        return pltpu.make_async_remote_copy(
            src_ref=to_right.at[step, index],
            dst_ref=target,
            send_sem=right_send.at[step, index],
            recv_sem=right_recv.at[step, index],
            device_id={"pair": right},
            device_id_type=MESH,
        )

    def send_left(step, index):
        if step == 0:
            target = lowers.at[index]
        else:
            target = out.at[pl.ds(index * chunk, chunk), pl.ds(width, width)]
        return pltpu.make_async_remote_copy(
            src_ref=to_left.at[step, index],
            dst_ref=target,
            send_sem=left_send.at[step, index],
            recv_sem=left_recv.at[step, index],
            device_id={"pair": left},
            device_id_type=MESH,
        )

    def exchange(step, offset):
        peer = lax.rem(row + offset, rows_axis)
        return pltpu.make_async_remote_copy(
            src_ref=crosses.at[step, row],
            dst_ref=crosses.at[step, row],
            send_sem=cross_send.at[step, offset - 1],
            recv_sem=cross_recv.at[step, offset - 1],
            device_id={"row": peer},
            device_id_type=MESH,
        )

    def start_left(index, carry):
        send_left(0, index).start()
        return carry

    def end_right(index, carry):
        send_right(0, index).wait_send()
        return carry

    for step in range(STEPS):

        def halves(index):
            if step == 0:
                return start[index, :, :width], start[index, :, width:]
            return uppers[index], lowers[index]

        def add_chunk(index, total):
            if step == 0:
                load(index).wait()
            else:

                @pl.when(jnp.logical_not(first))
                def _():
                    send_right(0, index).wait_recv()

                @pl.when(jnp.logical_not(last))
                def _():
                    send_left(0, index).wait_recv()

            return total + inner_rows(*halves(index))

        total = lax.fori_loop(0, CHUNKS - 1, add_chunk, jnp.zeros((width, width), F32))
        if step == 1:
            @pl.when(jnp.logical_not(odd))
            def _():
                pl.semaphore_wait(turn_sem, 1)

                @pl.when(jnp.logical_not(first))
                def _():
                    lax.fori_loop(0, CHUNKS, start_left, 0)

        total = add_chunk(CHUNKS - 1, total)
        crosses[step, row] = total
        if step == 0:
            neighbours = jnp.where(first, 0, 1) + jnp.where(last, 0, 1)
            pl.semaphore_wait(barrier, rows_axis - 1 + neighbours)
        copies = [exchange(step, offset) for offset in range(1, rows_axis)]
        if step == 0:

            @pl.when(jnp.logical_not(odd))
            def _():
                pl.semaphore_wait(first_sem, 1)

        for copy in copies:
            copy.start()
        for copy in copies:
            copy.wait()
        if step == 0:

            @pl.when(odd)
            def _():
                pl.semaphore_signal(first_sem, inc=1, device_id={"pair": left}, device_id_type=MESH)

        cross = crosses[step, 0]
        for index in range(1, rows_axis):
            cross = cross + crosses[step, index]
        for part, value in enumerate(split(rotation(cross, signs[step]))):
            weights[part] = value

        def turn_chunk(index, carry):
            upper, lower = halves(index)
            parts = split(jnp.concatenate([upper, lower], axis=1))
            turned = product(parts, (weights[0], weights[1]))
            new_upper, new_lower = turned[:, :width], turned[:, width:]
            to_right[step, index] = jnp.where(first, new_lower, new_upper)
            to_left[step, index] = new_lower

            @pl.when(jnp.logical_not(last))
            def _():
                send_right(step, index).start()

            @pl.when(odd if step == 0 else jnp.logical_not(first))
            def _():
                send_left(step, index).start()

            @pl.when(first)
            def _():
                if step == STEPS - 1:
                    out[pl.ds(index * chunk, chunk), :width] = new_upper
                else:
                    uppers[index] = new_upper

            @pl.when(last)
            def _():
                if step == STEPS - 1:
                    out[pl.ds(index * chunk, chunk), width:] = new_upper
                else:
                    lowers[index] = new_upper

            return carry

        lax.fori_loop(0, CHUNKS, turn_chunk, 0)
        if step == 0:

            @pl.when(odd)
            def _():
                @pl.when(jnp.logical_not(last))
                def _():
                    lax.fori_loop(0, CHUNKS - 1, end_right, 0)

                pl.semaphore_signal(turn_sem, inc=1, device_id={"pair": left}, device_id_type=MESH)

                @pl.when(jnp.logical_not(last))
                def _():
                    end_right(CHUNKS - 1, 0)

    def finish(index, carry):
        @pl.when(jnp.logical_not(last))
        def _():
            @pl.when(jnp.logical_not(odd))
            def _():
                send_right(0, index).wait_send()

            send_right(1, index).wait_send()
            send_left(1, index).wait_recv()

        @pl.when(jnp.logical_not(first))
        def _():
            send_left(0, index).wait_send()
            send_left(1, index).wait_send()
            send_right(1, index).wait_recv()

        return carry

    lax.fori_loop(0, CHUNKS, finish, 0)


def solution(mesh):
    rows_axis, pairs = mesh.shape["row"], mesh.shape["pair"]

    def per_device(panel, slot_block):
        rows, width = panel.shape[0], panel.shape[1] // 2
        chunk = rows // CHUNKS
        dma = pltpu.SemaphoreType.DMA
        return pl.pallas_call(
            functools.partial(kernel, rows_axis, pairs),
            out_shape=pltpu.VMEM(panel.shape, panel.dtype),
            in_specs=[
                pl.BlockSpec(memory_space=pltpu.SMEM),
                pl.BlockSpec(memory_space=pltpu.HBM),
            ],
            out_specs=pl.BlockSpec(memory_space=pltpu.VMEM),
            scratch_shapes=[
                pltpu.VMEM((CHUNKS, chunk, 2 * width), F32),
                pltpu.VMEM((CHUNKS, chunk, width), F32),
                pltpu.VMEM((CHUNKS, chunk, width), F32),
                pltpu.VMEM((STEPS, CHUNKS, chunk, width), F32),
                pltpu.VMEM((STEPS, CHUNKS, chunk, width), F32),
                pltpu.VMEM((2, 2 * width, 2 * width), BF16),
                pltpu.VMEM((STEPS, rows_axis, width, width), F32),
                dma((CHUNKS,)),
                dma((STEPS, max(1, rows_axis - 1))),
                dma((STEPS, max(1, rows_axis - 1))),
                dma((STEPS, CHUNKS)),
                dma((STEPS, CHUNKS)),
                dma((STEPS, CHUNKS)),
                dma((STEPS, CHUNKS)),
                pltpu.SemaphoreType.REGULAR,
                pltpu.SemaphoreType.REGULAR,
            ],
            compiler_params=pltpu.CompilerParams(collective_id=0, has_side_effects=True, vmem_limit_bytes=67043328 - 3 * panel.size * 4 // 2),
        )(slot_block, panel)

    return jax.shard_map(
        per_device,
        mesh=mesh,
        in_specs=(P("row", "pair"), P()),
        out_specs=P("row", "pair"),
        check_vma=False,
    )
```

```python
import functools
import math

import jax
import jax.numpy as jnp
from jax import lax
from jax.experimental import pallas as pl
from jax.experimental.pallas import tpu as pltpu
from jax.sharding import PartitionSpec as P

STEPS = 2
NS_ITERS = 3
CHUNKS = 8
RAW = 2
MESH = pl.DeviceIdType.MESH
F32 = jnp.float32
BF16 = jnp.bfloat16


def split(value):
    high = value.astype(BF16)
    return high, (value - high.astype(F32)).astype(BF16)


def raw_dot(a, b):
    return jnp.dot(a, b, preferred_element_type=F32)


def product(a, b):
    (a_high, a_low), (b_high, b_low) = a, b
    return raw_dot(a_high, b_high) + (raw_dot(a_high, b_low) + raw_dot(a_low, b_high))


def inner_rows(upper, lower):
    width = upper.shape[1]
    both = lax.dot_general(
        jnp.concatenate(split(upper), axis=1),
        jnp.concatenate(split(lower), axis=1),
        (((0,), (0,)), ((), ())),
        preferred_element_type=F32,
    )
    small = both[:width, width:] + both[width:, :width] + both[width:, width:]
    return both[:width, :width] + small


def identity_of(size):
    rows = lax.broadcasted_iota(jnp.int32, (size, size), 0)
    columns = lax.broadcasted_iota(jnp.int32, (size, size), 1)
    return jnp.where(rows == columns, 1.0, 0.0).astype(F32)


def rotation(cross, sign):
    identity = identity_of(cross.shape[0])
    scale = 2.0 * lax.rsqrt(jnp.sum(cross * cross, keepdims=True) + 1e-06)
    turned = cross.T
    plain_parts, turned_parts = split(cross), split(turned)
    sides = ((plain_parts, turned_parts), (turned_parts, plain_parts))
    iterates = [0.2 * identity + (0.2 * scale * scale) * product(a, b) for a, b in sides]
    factors = [1.5 * identity - 0.5 * value for value in iterates]
    roots = list(factors)
    for sweep in range(1, NS_ITERS):
        parts = [split(value) for value in factors]
        squares = [product(value, value) for value in parts]
        iterates = [product(split(a), split(b)) for a, b in zip(iterates, squares)]
        factors = [1.5 * identity - 0.5 * value for value in iterates]
        if sweep < NS_ITERS - 1:
            roots = [product(split(a), split(b)) for a, b in zip(roots, factors)]
    root_parts = [split(value * (1.0 / math.sqrt(5.0))) for value in roots]
    mixed = [
        split((sign * scale) * product(turned_parts, root_parts[0])),
        split((-sign * scale) * product(plain_parts, root_parts[1])),
    ]
    last_parts = [split(value) for value in factors]
    left_inverse, right_inverse = (product(a, b) for a, b in zip(root_parts, last_parts))
    from_lower, from_upper = (product(a, b) for a, b in zip(mixed, last_parts))
    return jnp.concatenate(
        [
            jnp.concatenate([left_inverse, from_upper], axis=1),
            jnp.concatenate([from_lower, right_inverse], axis=1),
        ],
        axis=0,
    )


def kernel(
    rows_axis, pairs, ids, panel, out,
    start, uppers, lowers, raw, mine, theirs, their_weights, to_right, to_left, weights, crosses,
    load_sem, cross_send, cross_recv, right_send, right_recv, left_send, left_recv, raw_send, raw_recv, turn_sem, first_sem,
):
    width = panel.shape[1] // 2
    chunk = panel.shape[0] // CHUNKS
    position = lax.axis_index("pair")
    row = lax.axis_index("row")
    first, last = position == 0, position == pairs - 1
    odd = lax.rem(position, 2) == 1
    even = jnp.logical_not(odd)
    sends_raw = jnp.logical_and(odd, jnp.logical_not(last))
    takes_raw = jnp.logical_and(even, jnp.logical_not(first))
    right, left = lax.rem(position + 1, pairs), lax.rem(position + pairs - 1, pairs)

    def load(index):
        return pltpu.make_async_copy(
            panel.at[pl.ds(index * chunk, chunk), :], start.at[index], load_sem.at[index]
        )

    def start_load(index, carry):
        load(index).start()
        return carry

    lax.fori_loop(0, CHUNKS, start_load, 0)

    barrier = pltpu.get_barrier_semaphore()
    for offset in range(1, rows_axis):
        peer = lax.rem(row + offset, rows_axis)
        pl.semaphore_signal(barrier, inc=1, device_id={"row": peer}, device_id_type=MESH)

    @pl.when(jnp.logical_not(first))
    def _():
        pl.semaphore_signal(barrier, inc=1, device_id={"pair": left}, device_id_type=MESH)

    @pl.when(jnp.logical_not(last))
    def _():
        pl.semaphore_signal(barrier, inc=1, device_id={"pair": right}, device_id_type=MESH)

    neighbours = jnp.where(first, 0, 1) + jnp.where(last, 0, 1)
    pl.semaphore_wait(barrier, rows_axis - 1 + neighbours)

    def send_raw(index):
        return pltpu.make_async_remote_copy(
            src_ref=start.at[index],
            dst_ref=raw.at[index],
            send_sem=raw_send.at[index],
            recv_sem=raw_recv.at[index],
            device_id={"pair": right},
            device_id_type=MESH,
        )

    def send_cross():
        return pltpu.make_async_remote_copy(
            src_ref=mine,
            dst_ref=theirs,
            send_sem=raw_send.at[RAW],
            recv_sem=raw_recv.at[RAW],
            device_id={"pair": right},
            device_id_type=MESH,
        )

    for index in range(RAW):
        load(index).wait()

        @pl.when(sends_raw)
        def _():
            send_raw(index).start()

    def sign_of(upper_id, lower_id):
        return jnp.where(upper_id < lower_id, 1.0, -1.0).astype(F32)

    moved_upper = jnp.where(first, ids[0], jnp.where(position == 1, ids[pairs], ids[left]))
    moved_lower = jnp.where(last, ids[pairs - 1], ids[pairs + right])
    signs = (
        sign_of(ids[position], ids[pairs + position]),
        sign_of(moved_upper, moved_lower),
    )
    left_sign = sign_of(ids[left], ids[pairs + left])

    def send_right(step, index):
        if step == 0:
            target = uppers.at[index]
        else:
            target = out.at[pl.ds(index * chunk, chunk), pl.ds(0, width)]
        return pltpu.make_async_remote_copy(
            src_ref=to_right.at[step, index],
            dst_ref=target,
            send_sem=right_send.at[step, index],
            recv_sem=right_recv.at[step, index],
            device_id={"pair": right},
            device_id_type=MESH,
        )

    def send_left(step, index):
        if step == 0:
            target = lowers.at[index]
        else:
            target = out.at[pl.ds(index * chunk, chunk), pl.ds(width, width)]
        return pltpu.make_async_remote_copy(
            src_ref=to_left.at[step, index],
            dst_ref=target,
            send_sem=left_send.at[step, index],
            recv_sem=left_recv.at[step, index],
            device_id={"pair": left},
            device_id_type=MESH,
        )

    def exchange(step, offset):
        peer = lax.rem(row + offset, rows_axis)
        return pltpu.make_async_remote_copy(
            src_ref=crosses.at[step, row],
            dst_ref=crosses.at[step, row],
            send_sem=cross_send.at[step, offset - 1],
            recv_sem=cross_recv.at[step, offset - 1],
            device_id={"row": peer},
            device_id_type=MESH,
        )

    def start_left(index, carry):
        send_left(0, index).start()
        return carry

    def end_right(index, carry):
        send_right(0, index).wait_send()
        return carry

    for step in range(STEPS):

        def halves(index):
            if step == 0:
                return start[index, :, :width], start[index, :, width:]
            return uppers[index], lowers[index]

        def add_chunk(index, total):
            if step == 0:

                @pl.when(index >= RAW)
                def _():
                    load(index).wait()

            else:

                @pl.when(jnp.logical_and(jnp.logical_not(first), jnp.logical_or(odd, index >= RAW)))
                def _():
                    send_right(0, index).wait_recv()

                @pl.when(jnp.logical_not(last))
                def _():
                    send_left(0, index).wait_recv()

            return total + inner_rows(*halves(index))

        total = lax.fori_loop(0, CHUNKS - 1, add_chunk, jnp.zeros((width, width), F32))
        if step == 1:
            @pl.when(jnp.logical_not(odd))
            def _():
                pl.semaphore_wait(turn_sem, 1)

                @pl.when(jnp.logical_not(first))
                def _():
                    lax.fori_loop(0, CHUNKS, start_left, 0)

        total = add_chunk(CHUNKS - 1, total)
        crosses[step, row] = total
        copies = [exchange(step, offset) for offset in range(1, rows_axis)]
        if step == 0:

            @pl.when(jnp.logical_not(odd))
            def _():
                pl.semaphore_wait(first_sem, 1)

        for copy in copies:
            copy.start()
        for copy in copies:
            copy.wait()
        if step == 0:

            @pl.when(odd)
            def _():
                pl.semaphore_signal(first_sem, inc=1, device_id={"pair": left}, device_id_type=MESH)

        cross = crosses[step, 0]
        for index in range(1, rows_axis):
            cross = cross + crosses[step, index]
        if step == 0:

            @pl.when(sends_raw)
            def _():
                mine[...] = cross
                send_cross().start()

        for part, value in enumerate(split(rotation(cross, signs[step]))):
            weights[part] = value

        def turn_chunk(turn, carry):
            index = lax.rem(turn + RAW, CHUNKS) if step == 0 else turn
            upper, lower = halves(index)
            parts = split(jnp.concatenate([upper, lower], axis=1))
            turned = product(parts, (weights[0], weights[1]))
            new_upper, new_lower = turned[:, :width], turned[:, width:]
            to_right[step, index] = jnp.where(first, new_lower, new_upper)
            to_left[step, index] = new_lower

            sends = jnp.logical_not(last)
            if step == 0:
                sends = jnp.logical_and(sends, jnp.logical_or(even, index >= RAW))

            @pl.when(sends)
            def _():
                send_right(step, index).start()

            @pl.when(odd if step == 0 else jnp.logical_not(first))
            def _():
                send_left(step, index).start()

            @pl.when(first)
            def _():
                if step == STEPS - 1:
                    out[pl.ds(index * chunk, chunk), :width] = new_upper
                else:
                    uppers[index] = new_upper

            @pl.when(last)
            def _():
                if step == STEPS - 1:
                    out[pl.ds(index * chunk, chunk), width:] = new_upper
                else:
                    lowers[index] = new_upper

            return carry

        lax.fori_loop(0, CHUNKS, turn_chunk, 0)
        if step == 0:

            @pl.when(odd)
            def _():
                @pl.when(jnp.logical_not(last))
                def _():
                    lax.fori_loop(RAW, CHUNKS - 1, end_right, 0)

                pl.semaphore_signal(turn_sem, inc=1, device_id={"pair": left}, device_id_type=MESH)

                @pl.when(jnp.logical_not(last))
                def _():
                    end_right(CHUNKS - 1, 0)
                    send_cross().wait_send()
                    for index in range(RAW):
                        send_raw(index).wait_send()

            @pl.when(takes_raw)
            def _():
                send_cross().wait_recv()
                for part, value in enumerate(split(rotation(theirs[...], left_sign)[:, :width])):
                    their_weights[part] = value
                for index in range(RAW):
                    send_raw(index).wait_recv()
                    uppers[index] = product(split(raw[index]), (their_weights[0], their_weights[1]))

    def finish(index, carry):
        @pl.when(jnp.logical_not(last))
        def _():
            @pl.when(jnp.logical_not(odd))
            def _():
                send_right(0, index).wait_send()

            send_right(1, index).wait_send()
            send_left(1, index).wait_recv()

        @pl.when(jnp.logical_not(first))
        def _():
            send_left(0, index).wait_send()
            send_left(1, index).wait_send()
            send_right(1, index).wait_recv()

        return carry

    lax.fori_loop(0, CHUNKS, finish, 0)


def solution(mesh):
    rows_axis, pairs = mesh.shape["row"], mesh.shape["pair"]

    def per_device(panel, slot_block):
        rows, width = panel.shape[0], panel.shape[1] // 2
        chunk = rows // CHUNKS
        dma = pltpu.SemaphoreType.DMA
        return pl.pallas_call(
            functools.partial(kernel, rows_axis, pairs),
            out_shape=pltpu.VMEM(panel.shape, panel.dtype),
            in_specs=[
                pl.BlockSpec(memory_space=pltpu.SMEM),
                pl.BlockSpec(memory_space=pltpu.HBM),
            ],
            out_specs=pl.BlockSpec(memory_space=pltpu.VMEM),
            scratch_shapes=[
                pltpu.VMEM((CHUNKS, chunk, 2 * width), F32),
                pltpu.VMEM((CHUNKS, chunk, width), F32),
                pltpu.VMEM((CHUNKS, chunk, width), F32),
                pltpu.VMEM((RAW, chunk, 2 * width), F32),
                pltpu.VMEM((width, width), F32),
                pltpu.VMEM((width, width), F32),
                pltpu.VMEM((2, 2 * width, width), BF16),
                pltpu.VMEM((STEPS, CHUNKS, chunk, width), F32),
                pltpu.VMEM((STEPS, CHUNKS, chunk, width), F32),
                pltpu.VMEM((2, 2 * width, 2 * width), BF16),
                pltpu.VMEM((STEPS, rows_axis, width, width), F32),
                dma((CHUNKS,)),
                dma((STEPS, max(1, rows_axis - 1))),
                dma((STEPS, max(1, rows_axis - 1))),
                dma((STEPS, CHUNKS)),
                dma((STEPS, CHUNKS)),
                dma((STEPS, CHUNKS)),
                dma((STEPS, CHUNKS)),
                dma((RAW + 1,)),
                dma((RAW + 1,)),
                pltpu.SemaphoreType.REGULAR,
                pltpu.SemaphoreType.REGULAR,
            ],
            compiler_params=pltpu.CompilerParams(collective_id=0, has_side_effects=True, vmem_limit_bytes=67043328 - 3 * panel.size * 4 // 2),
        )(slot_block, panel)

    return jax.shard_map(
        per_device,
        mesh=mesh,
        in_specs=(P("row", "pair"), P()),
        out_specs=P("row", "pair"),
        check_vma=False,
    )
```

```python
import functools
import math

import jax
import jax.numpy as jnp
from jax import lax
from jax.experimental import pallas as pl
from jax.experimental.pallas import tpu as pltpu
from jax.sharding import PartitionSpec as P

STEPS = 2
NS_ITERS = 3
CHUNKS = 8
RAW = 2
MESH = pl.DeviceIdType.MESH
F32 = jnp.float32
BF16 = jnp.bfloat16


def split(value):
    high = value.astype(BF16)
    return high, (value - high.astype(F32)).astype(BF16)


def raw_dot(a, b):
    return jnp.dot(a, b, preferred_element_type=F32)


def product(a, b):
    (a_high, a_low), (b_high, b_low) = a, b
    return raw_dot(a_high, b_high) + (raw_dot(a_high, b_low) + raw_dot(a_low, b_high))


def inner_rows(upper, lower):
    width = upper.shape[1]
    both = lax.dot_general(
        jnp.concatenate(split(upper), axis=1),
        jnp.concatenate(split(lower), axis=1),
        (((0,), (0,)), ((), ())),
        preferred_element_type=F32,
    )
    small = both[:width, width:] + both[width:, :width] + both[width:, width:]
    return both[:width, :width] + small


def identity_of(size):
    rows = lax.broadcasted_iota(jnp.int32, (size, size), 0)
    columns = lax.broadcasted_iota(jnp.int32, (size, size), 1)
    return jnp.where(rows == columns, 1.0, 0.0).astype(F32)


def rotation(cross, sign):
    identity = identity_of(cross.shape[0])
    scale = 2.0 * lax.rsqrt(jnp.sum(cross * cross, keepdims=True) + 1e-06)
    turned = cross.T
    plain_parts, turned_parts = split(cross), split(turned)
    sides = ((plain_parts, turned_parts), (turned_parts, plain_parts))
    iterates = [0.2 * identity + (0.2 * scale * scale) * product(a, b) for a, b in sides]
    factors = [1.5 * identity - 0.5 * value for value in iterates]
    roots = list(factors)
    for sweep in range(1, NS_ITERS):
        parts = [split(value) for value in factors]
        squares = [product(value, value) for value in parts]
        iterates = [product(split(a), split(b)) for a, b in zip(iterates, squares)]
        factors = [1.5 * identity - 0.5 * value for value in iterates]
        if sweep < NS_ITERS - 1:
            roots = [product(split(a), split(b)) for a, b in zip(roots, factors)]
    root_parts = [split(value * (1.0 / math.sqrt(5.0))) for value in roots]
    mixed = [
        split((sign * scale) * product(turned_parts, root_parts[0])),
        split((-sign * scale) * product(plain_parts, root_parts[1])),
    ]
    last_parts = [split(value) for value in factors]
    left_inverse, right_inverse = (product(a, b) for a, b in zip(root_parts, last_parts))
    from_lower, from_upper = (product(a, b) for a, b in zip(mixed, last_parts))
    return jnp.concatenate(
        [
            jnp.concatenate([left_inverse, from_upper], axis=1),
            jnp.concatenate([from_lower, right_inverse], axis=1),
        ],
        axis=0,
    )


def kernel(
    rows_axis, pairs, ids, panel, out,
    start, uppers, lowers, raw, mine, theirs, their_weights, to_right, to_left, weights, crosses,
    load_sem, cross_send, cross_recv, right_send, right_recv, left_send, left_recv, raw_send, raw_recv, turn_sem, first_sem,
):
    width = panel.shape[1] // 2
    chunk = panel.shape[0] // CHUNKS
    position = lax.axis_index("pair")
    row = lax.axis_index("row")
    first, last = position == 0, position == pairs - 1
    odd = lax.rem(position, 2) == 1
    even = jnp.logical_not(odd)
    sends_raw = jnp.logical_and(odd, jnp.logical_not(last))
    takes_raw = jnp.logical_and(even, jnp.logical_not(first))
    right, left = lax.rem(position + 1, pairs), lax.rem(position + pairs - 1, pairs)

    def load(index):
        return pltpu.make_async_copy(
            panel.at[pl.ds(index * chunk, chunk), :], start.at[index], load_sem.at[index]
        )

    def start_load(index, carry):
        load(index).start()
        return carry

    lax.fori_loop(0, CHUNKS, start_load, 0)

    barrier = pltpu.get_barrier_semaphore()
    for offset in range(1, rows_axis):
        peer = lax.rem(row + offset, rows_axis)
        pl.semaphore_signal(barrier, inc=1, device_id={"row": peer}, device_id_type=MESH)

    @pl.when(jnp.logical_not(first))
    def _():
        pl.semaphore_signal(barrier, inc=1, device_id={"pair": left}, device_id_type=MESH)

    @pl.when(jnp.logical_not(last))
    def _():
        pl.semaphore_signal(barrier, inc=1, device_id={"pair": right}, device_id_type=MESH)

    neighbours = jnp.where(first, 0, 1) + jnp.where(last, 0, 1)

    def send_raw(index):
        return pltpu.make_async_remote_copy(
            src_ref=start.at[index],
            dst_ref=raw.at[index],
            send_sem=raw_send.at[index],
            recv_sem=raw_recv.at[index],
            device_id={"pair": right},
            device_id_type=MESH,
        )

    def send_cross():
        return pltpu.make_async_remote_copy(
            src_ref=mine,
            dst_ref=theirs,
            send_sem=raw_send.at[RAW],
            recv_sem=raw_recv.at[RAW],
            device_id={"pair": right},
            device_id_type=MESH,
        )

    def sign_of(upper_id, lower_id):
        return jnp.where(upper_id < lower_id, 1.0, -1.0).astype(F32)

    moved_upper = jnp.where(first, ids[0], jnp.where(position == 1, ids[pairs], ids[left]))
    moved_lower = jnp.where(last, ids[pairs - 1], ids[pairs + right])
    signs = (
        sign_of(ids[position], ids[pairs + position]),
        sign_of(moved_upper, moved_lower),
    )
    left_sign = sign_of(ids[left], ids[pairs + left])

    def send_right(step, index):
        if step == 0:
            target = uppers.at[index]
        else:
            target = out.at[pl.ds(index * chunk, chunk), pl.ds(0, width)]
        return pltpu.make_async_remote_copy(
            src_ref=to_right.at[step, index],
            dst_ref=target,
            send_sem=right_send.at[step, index],
            recv_sem=right_recv.at[step, index],
            device_id={"pair": right},
            device_id_type=MESH,
        )

    def send_left(step, index):
        if step == 0:
            target = lowers.at[index]
        else:
            target = out.at[pl.ds(index * chunk, chunk), pl.ds(width, width)]
        return pltpu.make_async_remote_copy(
            src_ref=to_left.at[step, index],
            dst_ref=target,
            send_sem=left_send.at[step, index],
            recv_sem=left_recv.at[step, index],
            device_id={"pair": left},
            device_id_type=MESH,
        )

    def exchange(step, offset):
        peer = lax.rem(row + offset, rows_axis)
        return pltpu.make_async_remote_copy(
            src_ref=crosses.at[step, row],
            dst_ref=crosses.at[step, row],
            send_sem=cross_send.at[step, offset - 1],
            recv_sem=cross_recv.at[step, offset - 1],
            device_id={"row": peer},
            device_id_type=MESH,
        )

    def start_left(index, carry):
        send_left(0, index).start()
        return carry

    def end_right(index, carry):
        send_right(0, index).wait_send()
        return carry

    for step in range(STEPS):

        def halves(index):
            if step == 0:
                return start[index, :, :width], start[index, :, width:]
            return uppers[index], lowers[index]

        def await_chunk(index):
            if step == 0:
                load(index).wait()
                return

            @pl.when(jnp.logical_not(first) if index >= RAW else jnp.logical_and(odd, jnp.logical_not(first)))
            def _():
                send_right(0, index).wait_recv()

            @pl.when(jnp.logical_not(last))
            def _():
                send_left(0, index).wait_recv()

        group = CHUNKS // 2 if step == 0 else CHUNKS // 4
        total = jnp.zeros((width, width), F32)
        for lead in range(0, CHUNKS, group):
            if step == 1 and lead == CHUNKS - group:
                @pl.when(even)
                def _():
                    pl.semaphore_wait(turn_sem, 1)

                    @pl.when(jnp.logical_not(first))
                    def _():
                        lax.fori_loop(0, CHUNKS, start_left, 0)

            for index in range(lead, lead + group):
                await_chunk(index)
            for index in range(lead, lead + group):
                total = total + inner_rows(*halves(index))
            if step == 0 and lead == 0:
                pl.semaphore_wait(barrier, rows_axis - 1 + neighbours)

                @pl.when(sends_raw)
                def _():
                    for index in range(RAW):
                        send_raw(index).start()

        crosses[step, row] = total
        copies = [exchange(step, offset) for offset in range(1, rows_axis)]
        if step == 0:

            @pl.when(jnp.logical_not(odd))
            def _():
                pl.semaphore_wait(first_sem, 1)

        for copy in copies:
            copy.start()
        for copy in copies:
            copy.wait()
        if step == 0:

            @pl.when(odd)
            def _():
                pl.semaphore_signal(first_sem, inc=1, device_id={"pair": left}, device_id_type=MESH)

        cross = crosses[step, 0]
        for index in range(1, rows_axis):
            cross = cross + crosses[step, index]
        if step == 0:

            @pl.when(sends_raw)
            def _():
                mine[...] = cross
                send_cross().start()

        for part, value in enumerate(split(rotation(cross, signs[step]))):
            weights[part] = value

        def turn_chunk(turn, carry):
            index = lax.rem(turn + RAW, CHUNKS) if step == 0 else turn
            upper, lower = halves(index)
            parts = split(jnp.concatenate([upper, lower], axis=1))
            turned = product(parts, (weights[0], weights[1]))
            new_upper, new_lower = turned[:, :width], turned[:, width:]
            to_right[step, index] = jnp.where(first, new_lower, new_upper)
            to_left[step, index] = new_lower

            sends = jnp.logical_not(last)
            if step == 0:
                sends = jnp.logical_and(sends, jnp.logical_or(even, index >= RAW))

            @pl.when(sends)
            def _():
                send_right(step, index).start()

            @pl.when(odd if step == 0 else jnp.logical_not(first))
            def _():
                send_left(step, index).start()

            @pl.when(first)
            def _():
                if step == STEPS - 1:
                    out[pl.ds(index * chunk, chunk), :width] = new_upper
                else:
                    uppers[index] = new_upper

            @pl.when(last)
            def _():
                if step == STEPS - 1:
                    out[pl.ds(index * chunk, chunk), width:] = new_upper
                else:
                    lowers[index] = new_upper

            return carry

        lax.fori_loop(0, CHUNKS, turn_chunk, 0)
        if step == 0:

            @pl.when(odd)
            def _():
                @pl.when(jnp.logical_not(last))
                def _():
                    lax.fori_loop(RAW, CHUNKS - 2, end_right, 0)

                pl.semaphore_signal(turn_sem, inc=1, device_id={"pair": left}, device_id_type=MESH)

                @pl.when(jnp.logical_not(last))
                def _():
                    end_right(CHUNKS - 2, 0)
                    end_right(CHUNKS - 1, 0)
                    send_cross().wait_send()
                    for index in range(RAW):
                        send_raw(index).wait_send()

            @pl.when(takes_raw)
            def _():
                send_cross().wait_recv()
                for part, value in enumerate(split(rotation(theirs[...], left_sign)[:, :width])):
                    their_weights[part] = value
                for index in range(RAW):
                    send_raw(index).wait_recv()
                    uppers[index] = product(split(raw[index]), (their_weights[0], their_weights[1]))

    def finish(index, carry):
        @pl.when(jnp.logical_not(last))
        def _():
            @pl.when(jnp.logical_not(odd))
            def _():
                send_right(0, index).wait_send()

            send_right(1, index).wait_send()
            send_left(1, index).wait_recv()

        @pl.when(jnp.logical_not(first))
        def _():
            send_left(0, index).wait_send()
            send_left(1, index).wait_send()
            send_right(1, index).wait_recv()

        return carry

    lax.fori_loop(0, CHUNKS, finish, 0)


def solution(mesh):
    rows_axis, pairs = mesh.shape["row"], mesh.shape["pair"]

    def per_device(panel, slot_block):
        rows, width = panel.shape[0], panel.shape[1] // 2
        chunk = rows // CHUNKS
        dma = pltpu.SemaphoreType.DMA
        return pl.pallas_call(
            functools.partial(kernel, rows_axis, pairs),
            out_shape=pltpu.VMEM(panel.shape, panel.dtype),
            in_specs=[
                pl.BlockSpec(memory_space=pltpu.SMEM),
                pl.BlockSpec(memory_space=pltpu.HBM),
            ],
            out_specs=pl.BlockSpec(memory_space=pltpu.VMEM),
            scratch_shapes=[
                pltpu.VMEM((CHUNKS, chunk, 2 * width), F32),
                pltpu.VMEM((CHUNKS, chunk, width), F32),
                pltpu.VMEM((CHUNKS, chunk, width), F32),
                pltpu.VMEM((RAW, chunk, 2 * width), F32),
                pltpu.VMEM((width, width), F32),
                pltpu.VMEM((width, width), F32),
                pltpu.VMEM((2, 2 * width, width), BF16),
                pltpu.VMEM((STEPS, CHUNKS, chunk, width), F32),
                pltpu.VMEM((STEPS, CHUNKS, chunk, width), F32),
                pltpu.VMEM((2, 2 * width, 2 * width), BF16),
                pltpu.VMEM((STEPS, rows_axis, width, width), F32),
                dma((CHUNKS,)),
                dma((STEPS, max(1, rows_axis - 1))),
                dma((STEPS, max(1, rows_axis - 1))),
                dma((STEPS, CHUNKS)),
                dma((STEPS, CHUNKS)),
                dma((STEPS, CHUNKS)),
                dma((STEPS, CHUNKS)),
                dma((RAW + 1,)),
                dma((RAW + 1,)),
                pltpu.SemaphoreType.REGULAR,
                pltpu.SemaphoreType.REGULAR,
            ],
            compiler_params=pltpu.CompilerParams(collective_id=0, has_side_effects=True, vmem_limit_bytes=67043328 - 3 * panel.size * 4 // 2),
        )(slot_block, panel)

    return jax.shard_map(
        per_device,
        mesh=mesh,
        in_specs=(P("row", "pair"), P()),
        out_specs=P("row", "pair"),
        check_vma=False,
    )
```

```python
import functools
import math

import jax
import jax.numpy as jnp
from jax import lax
from jax.experimental import pallas as pl
from jax.experimental.pallas import tpu as pltpu
from jax.sharding import PartitionSpec as P

STEPS = 2
NS_ITERS = 3
CHUNKS = 4
RAW = 1
MESH = pl.DeviceIdType.MESH
F32 = jnp.float32
BF16 = jnp.bfloat16


def split(value):
    high = value.astype(BF16)
    return high, (value - high.astype(F32)).astype(BF16)


def raw_dot(a, b):
    return jnp.dot(a, b, preferred_element_type=F32)


def product(a, b):
    (a_high, a_low), (b_high, b_low) = a, b
    return raw_dot(a_high, b_high) + (raw_dot(a_high, b_low) + raw_dot(a_low, b_high))


def inner_rows(upper, lower):
    width = upper.shape[1]
    both = lax.dot_general(
        jnp.concatenate(split(upper), axis=1),
        jnp.concatenate(split(lower), axis=1),
        (((0,), (0,)), ((), ())),
        preferred_element_type=F32,
    )
    small = both[:width, width:] + both[width:, :width] + both[width:, width:]
    return both[:width, :width] + small


def identity_of(size):
    rows = lax.broadcasted_iota(jnp.int32, (size, size), 0)
    columns = lax.broadcasted_iota(jnp.int32, (size, size), 1)
    return jnp.where(rows == columns, 1.0, 0.0).astype(F32)


def rotation(cross, sign):
    identity = identity_of(cross.shape[0])
    scale = 2.0 * lax.rsqrt(jnp.sum(cross * cross, keepdims=True) + 1e-06)
    turned = cross.T
    plain_parts, turned_parts = split(cross), split(turned)
    sides = ((plain_parts, turned_parts), (turned_parts, plain_parts))
    iterates = [0.2 * identity + (0.2 * scale * scale) * product(a, b) for a, b in sides]
    factors = [1.5 * identity - 0.5 * value for value in iterates]
    roots = list(factors)
    for sweep in range(1, NS_ITERS):
        parts = [split(value) for value in factors]
        squares = [product(value, value) for value in parts]
        iterates = [product(split(a), split(b)) for a, b in zip(iterates, squares)]
        factors = [1.5 * identity - 0.5 * value for value in iterates]
        if sweep < NS_ITERS - 1:
            roots = [product(split(a), split(b)) for a, b in zip(roots, factors)]
    root_parts = [split(value * (1.0 / math.sqrt(5.0))) for value in roots]
    mixed = [
        split((sign * scale) * product(turned_parts, root_parts[0])),
        split((-sign * scale) * product(plain_parts, root_parts[1])),
    ]
    last_parts = [split(value) for value in factors]
    left_inverse, right_inverse = (product(a, b) for a, b in zip(root_parts, last_parts))
    from_lower, from_upper = (product(a, b) for a, b in zip(mixed, last_parts))
    return jnp.concatenate(
        [
            jnp.concatenate([left_inverse, from_upper], axis=1),
            jnp.concatenate([from_lower, right_inverse], axis=1),
        ],
        axis=0,
    )


def kernel(
    rows_axis, pairs, ids, panel, out,
    start, uppers, lowers, raw, mine, theirs, their_weights, to_right, to_left, landed, weights, crosses,
    load_sem, cross_send, cross_recv, right_send, right_recv, left_send, left_recv, raw_send, raw_recv, turn_sem, first_sem,
):
    width = panel.shape[1] // 2
    chunk = panel.shape[0] // CHUNKS
    position = lax.axis_index("pair")
    row = lax.axis_index("row")
    first, last = position == 0, position == pairs - 1
    odd = lax.rem(position, 2) == 1
    even = jnp.logical_not(odd)
    sends_raw = jnp.logical_and(odd, jnp.logical_not(last))
    takes_raw = jnp.logical_and(even, jnp.logical_not(first))
    right, left = lax.rem(position + 1, pairs), lax.rem(position + pairs - 1, pairs)

    def load(index):
        return pltpu.make_async_copy(
            panel.at[pl.ds(index * chunk, chunk), :], start.at[index], load_sem.at[index]
        )

    def start_load(index, carry):
        load(index).start()
        return carry

    lax.fori_loop(0, CHUNKS, start_load, 0)

    barrier = pltpu.get_barrier_semaphore()
    for offset in range(1, rows_axis):
        peer = lax.rem(row + offset, rows_axis)
        pl.semaphore_signal(barrier, inc=1, device_id={"row": peer}, device_id_type=MESH)

    @pl.when(jnp.logical_not(first))
    def _():
        pl.semaphore_signal(barrier, inc=1, device_id={"pair": left}, device_id_type=MESH)

    @pl.when(jnp.logical_not(last))
    def _():
        pl.semaphore_signal(barrier, inc=1, device_id={"pair": right}, device_id_type=MESH)

    neighbours = jnp.where(first, 0, 1) + jnp.where(last, 0, 1)

    def send_raw(index):
        return pltpu.make_async_remote_copy(
            src_ref=start.at[index],
            dst_ref=raw.at[index],
            send_sem=raw_send.at[index],
            recv_sem=raw_recv.at[index],
            device_id={"pair": right},
            device_id_type=MESH,
        )

    def send_cross():
        return pltpu.make_async_remote_copy(
            src_ref=mine,
            dst_ref=theirs,
            send_sem=raw_send.at[RAW],
            recv_sem=raw_recv.at[RAW],
            device_id={"pair": right},
            device_id_type=MESH,
        )

    def sign_of(upper_id, lower_id):
        return jnp.where(upper_id < lower_id, 1.0, -1.0).astype(F32)

    moved_upper = jnp.where(first, ids[0], jnp.where(position == 1, ids[pairs], ids[left]))
    moved_lower = jnp.where(last, ids[pairs - 1], ids[pairs + right])
    signs = (
        sign_of(ids[position], ids[pairs + position]),
        sign_of(moved_upper, moved_lower),
    )
    left_sign = sign_of(ids[left], ids[pairs + left])

    def send_right(step, index):
        if step == 0:
            target = uppers.at[index]
        else:
            target = landed.at[0, index]
        return pltpu.make_async_remote_copy(
            src_ref=to_right.at[step, index],
            dst_ref=target,
            send_sem=right_send.at[step, index],
            recv_sem=right_recv.at[step, index],
            device_id={"pair": right},
            device_id_type=MESH,
        )

    def send_left(step, index):
        if step == 0:
            target = lowers.at[index]
        else:
            target = landed.at[1, index]
        return pltpu.make_async_remote_copy(
            src_ref=to_left.at[step, index],
            dst_ref=target,
            send_sem=left_send.at[step, index],
            recv_sem=left_recv.at[step, index],
            device_id={"pair": left},
            device_id_type=MESH,
        )

    def exchange(step, offset):
        peer = lax.rem(row + offset, rows_axis)
        return pltpu.make_async_remote_copy(
            src_ref=crosses.at[step, row],
            dst_ref=crosses.at[step, row],
            send_sem=cross_send.at[step, offset - 1],
            recv_sem=cross_recv.at[step, offset - 1],
            device_id={"row": peer},
            device_id_type=MESH,
        )

    def start_left(index, carry):
        send_left(0, index).start()
        return carry

    def end_right(index, carry):
        send_right(0, index).wait_send()
        return carry

    for step in range(STEPS):

        def halves(index):
            if step == 0:
                return start[index, :, :width], start[index, :, width:]
            return uppers[index], lowers[index]

        def await_chunk(index):
            if step == 0:
                load(index).wait()
                return

            @pl.when(jnp.logical_not(first) if index >= RAW else jnp.logical_and(odd, jnp.logical_not(first)))
            def _():
                send_right(0, index).wait_recv()

            @pl.when(jnp.logical_not(last))
            def _():
                send_left(0, index).wait_recv()

        group = CHUNKS // 2 if step == 0 else CHUNKS // 4
        total = jnp.zeros((width, width), F32)
        for lead in range(0, CHUNKS, group):
            if step == 1 and lead == CHUNKS - group:
                @pl.when(even)
                def _():
                    pl.semaphore_wait(turn_sem, 1)

                    @pl.when(jnp.logical_not(first))
                    def _():
                        lax.fori_loop(0, CHUNKS, start_left, 0)

            for index in range(lead, lead + group):
                await_chunk(index)
            for index in range(lead, lead + group):
                total = total + inner_rows(*halves(index))
            if step == 0 and lead == 0:
                pl.semaphore_wait(barrier, rows_axis - 1 + neighbours)

                @pl.when(sends_raw)
                def _():
                    for index in range(RAW):
                        send_raw(index).start()

        crosses[step, row] = total
        copies = [exchange(step, offset) for offset in range(1, rows_axis)]
        if step == 0:

            @pl.when(jnp.logical_not(odd))
            def _():
                pl.semaphore_wait(first_sem, 1)

        for copy in copies:
            copy.start()
        for copy in copies:
            copy.wait()
        if step == 0:

            @pl.when(odd)
            def _():
                pl.semaphore_signal(first_sem, inc=1, device_id={"pair": left}, device_id_type=MESH)

        cross = crosses[step, 0]
        for index in range(1, rows_axis):
            cross = cross + crosses[step, index]
        if step == 0:

            @pl.when(sends_raw)
            def _():
                mine[...] = cross
                send_cross().start()

        for part, value in enumerate(split(rotation(cross, signs[step]))):
            weights[part] = value

        def turn_chunk(turn, carry):
            index = lax.rem(turn + RAW, CHUNKS) if step == 0 else turn
            upper, lower = halves(index)
            parts = split(jnp.concatenate([upper, lower], axis=1))
            turned = product(parts, (weights[0], weights[1]))
            new_upper, new_lower = turned[:, :width], turned[:, width:]
            to_right[step, index] = jnp.where(first, new_lower, new_upper)
            to_left[step, index] = new_lower

            sends = jnp.logical_not(last)
            if step == 0:
                sends = jnp.logical_and(sends, jnp.logical_or(even, index >= RAW))

            @pl.when(sends)
            def _():
                send_right(step, index).start()

            @pl.when(odd if step == 0 else jnp.logical_not(first))
            def _():
                send_left(step, index).start()

            @pl.when(first)
            def _():
                if step == STEPS - 1:
                    out[pl.ds(index * chunk, chunk), :width] = new_upper
                else:
                    uppers[index] = new_upper

            @pl.when(last)
            def _():
                if step == STEPS - 1:
                    out[pl.ds(index * chunk, chunk), width:] = new_upper
                else:
                    lowers[index] = new_upper

            return carry

        lax.fori_loop(0, CHUNKS, turn_chunk, 0)
        if step == 0:

            @pl.when(odd)
            def _():
                @pl.when(jnp.logical_not(last))
                def _():
                    lax.fori_loop(RAW, CHUNKS - CHUNKS // 4, end_right, 0)

                pl.semaphore_signal(turn_sem, inc=1, device_id={"pair": left}, device_id_type=MESH)

                @pl.when(jnp.logical_not(last))
                def _():
                    lax.fori_loop(CHUNKS - CHUNKS // 4, CHUNKS, end_right, 0)
                    send_cross().wait_send()
                    for index in range(RAW):
                        send_raw(index).wait_send()

            @pl.when(takes_raw)
            def _():
                send_cross().wait_recv()
                for part, value in enumerate(split(rotation(theirs[...], left_sign)[:, :width])):
                    their_weights[part] = value
                for index in range(RAW):
                    send_raw(index).wait_recv()
                    uppers[index] = product(split(raw[index]), (their_weights[0], their_weights[1]))

    def finish(index, carry):
        @pl.when(jnp.logical_not(last))
        def _():
            @pl.when(jnp.logical_not(odd))
            def _():
                send_right(0, index).wait_send()

            send_right(1, index).wait_send()
            send_left(1, index).wait_recv()
            out[pl.ds(index * chunk, chunk), width:] = landed[1, index]

        @pl.when(jnp.logical_not(first))
        def _():
            send_left(0, index).wait_send()
            send_left(1, index).wait_send()
            send_right(1, index).wait_recv()
            out[pl.ds(index * chunk, chunk), :width] = landed[0, index]

        return carry

    lax.fori_loop(0, CHUNKS, finish, 0)


def solution(mesh):
    rows_axis, pairs = mesh.shape["row"], mesh.shape["pair"]

    def per_device(panel, slot_block):
        rows, width = panel.shape[0], panel.shape[1] // 2
        chunk = rows // CHUNKS
        dma = pltpu.SemaphoreType.DMA
        return pl.pallas_call(
            functools.partial(kernel, rows_axis, pairs),
            out_shape=pltpu.VMEM(panel.shape, panel.dtype),
            in_specs=[
                pl.BlockSpec(memory_space=pltpu.SMEM),
                pl.BlockSpec(memory_space=pltpu.HBM),
            ],
            out_specs=pl.BlockSpec(memory_space=pltpu.VMEM),
            scratch_shapes=[
                pltpu.VMEM((CHUNKS, chunk, 2 * width), F32),
                pltpu.VMEM((CHUNKS, chunk, width), F32),
                pltpu.VMEM((CHUNKS, chunk, width), F32),
                pltpu.VMEM((RAW, chunk, 2 * width), F32),
                pltpu.VMEM((width, width), F32),
                pltpu.VMEM((width, width), F32),
                pltpu.VMEM((2, 2 * width, width), BF16),
                pltpu.VMEM((STEPS, CHUNKS, chunk, width), F32),
                pltpu.VMEM((STEPS, CHUNKS, chunk, width), F32),
                pltpu.VMEM((2, CHUNKS, chunk, width), F32),
                pltpu.VMEM((2, 2 * width, 2 * width), BF16),
                pltpu.VMEM((STEPS, rows_axis, width, width), F32),
                dma((CHUNKS,)),
                dma((STEPS, max(1, rows_axis - 1))),
                dma((STEPS, max(1, rows_axis - 1))),
                dma((STEPS, CHUNKS)),
                dma((STEPS, CHUNKS)),
                dma((STEPS, CHUNKS)),
                dma((STEPS, CHUNKS)),
                dma((RAW + 1,)),
                dma((RAW + 1,)),
                pltpu.SemaphoreType.REGULAR,
                pltpu.SemaphoreType.REGULAR,
            ],
            compiler_params=pltpu.CompilerParams(collective_id=0, has_side_effects=True, vmem_limit_bytes=67043328 - 3 * panel.size * 4 // 2),
        )(slot_block, panel)

    return jax.shard_map(
        per_device,
        mesh=mesh,
        in_specs=(P("row", "pair"), P()),
        out_specs=P("row", "pair"),
        check_vma=False,
    )
```
